256 devices in a mesh: dp: 16 (over x_hi, y, core), hid: 16 (over x_lo, z).
Axes of the slice: x: 4 (x_hi: 2, x_lo: 2; x = x_hi * 2 + x_lo), y: 4, z: 8, core: 2. Of those that a mesh axis runs over, the one named last changes fastest.
Arguments:
- tokens: bfloat16 [2048, 4096], P('dp', 'hid'), may hold values from -6 to 6
- expert_ids: int32 [2048, 2], P('dp'), may hold values from 0 to 7, all different within a row; in each aligned block of 128 rows (0 to 127, 128 to 255, ...) at most 48 rows name the same one
- gate_levels: int32 [2048, 2], P('dp'), may hold values from 1 to 255
- w_gate: bfloat16 [4096, 114688], P(None, ('dp', 'hid')), may hold values from -0.09375 to 0.09375
- w_up: bfloat16 [4096, 114688], P(None, ('dp', 'hid')), may hold values from -0.09375 to 0.09375
- w_down: bfloat16 [114688, 4096], P(('dp', 'hid')), may hold values from -0.046875 to 0.046875
Outputs:
- mixed: bfloat16 [2048, 4096], P('dp', 'hid')
The draws below stay inside these ranges and needn't reach their ends.
Inputs may be any that keep to these rules, and one draw needn't show every extreme that they name: `expert_ids`: each row names two different experts. Among the 128 rows of one index of dp no expert is named by more than 48 rows, and in some such block one expert is named by exactly 48 rows.
All inputs are finite; a program needn't handle non-finite values.
Results may differ from the reference program's by a relative error of at most 0.019.
Values may be sent and summed in bfloat16 or wider, within the bound.
A program may use at most 64 MiB of HBM per device.

```python
import math
import jax
import jax.numpy as jnp
import numpy as np
from jax import lax

D = 4096
FF = 14336
EXPERTS = 8
TOK_DP = 128
TOKENS = 2048
CAP = 48
FSPLIT = 2
FB = 448
N_DP = 16
N_HID = 16


def touch_ends(values, key, low, top_value):
    shape = values.shape
    place = [jax.random.randint(jax.random.fold_in(key, axis), (), 0, shape[axis]) for axis in range(len(shape))]
    values = values.at[tuple(place)].set(low)
    longest = shape.index(max(shape))
    place[longest] = (place[longest] + 1) % shape[longest]
    return values.at[tuple(place)].set(top_value)


def shard_levels(own_key, dims, shards, low, largest):
    level = 1.0
    for position, blocks in shards:
        heights = jax.random.uniform(jax.random.fold_in(jax.random.fold_in(own_key, 6), position), (blocks,), jnp.float32, low / len(shards), largest / len(shards))
        level = level * jnp.repeat(jnp.exp(heights), dims[position] // blocks).reshape((-1,) + (1,) * (len(dims) - 1 - position))
    return level


def routed_block(stream_key, own, number, rows, count, top, most, lean):
    ranking = jax.random.permutation(stream_key, count)
    heavy_load, ordinary = load_shares(count, rows * top, most, lean, True), load_shares(count, rows * top, most, lean, False)
    places = jnp.arange(count)

    def named(tallies, turn):
        used = int((tallies > 0).sum())
        fixed = max(1, used // 4)
        moved = fixed + (places - fixed + turn * (used - fixed)) % max(1, count - fixed)
        return jnp.zeros((count,), jnp.int32).at[ranking[jnp.where(places < fixed, places, moved)]].set(jnp.asarray(tallies, jnp.int32))

    tallies = jnp.where(number % 4 == 0, named(heavy_load, number // 4), named(ordinary, number - number // 4 - 1))
    mixed = jax.random.permutation(jax.random.fold_in(own, 3), count)
    source_of, receiver = mixed[0:count // 2 * 2:2], mixed[1:count // 2 * 2:2]
    room = jnp.minimum(tallies[source_of] - 1, most - tallies[receiver]) // 2
    room = jnp.where((source_of == ranking[0]) | (receiver == ranking[0]) | (tallies[receiver] == 0), 0, jnp.maximum(room, 0))
    moved = jax.random.randint(jax.random.fold_in(own, 4), (count // 2,), 0, 1 << 20) % (room + 1)
    tallies = tallies.at[source_of].add(-moved).at[receiver].add(moved)
    labels = jnp.searchsorted(jnp.cumsum(tallies), jnp.arange(rows * top), side="right").astype(jnp.int32)
    table = labels.reshape(top, rows).T
    table = table[jax.random.permutation(jax.random.fold_in(own, 1), rows)]
    turn = jax.random.randint(jax.random.fold_in(own, 2), (rows, 1), 0, top)
    return jnp.take_along_axis(table, (jnp.arange(top)[None, :] + turn) % top, axis=1)


def load_shares(amount, total, reach, skew, full):
    loads = [(1 << 20) // math.isqrt(grade ** skew) + 1 for grade in range(1, amount + 1)]
    largest = reach if full else min(reach, max(-(-total // amount), total * loads[0] // sum(loads)))
    least = 1 if total - largest >= amount - 1 else 0
    given, rest = [largest] + [least] * (amount - 1), total - largest - least * (amount - 1)
    while rest > 0:
        movable = [i for i in range(1, amount) if given[i] < largest] or [i for i in range(1, amount) if given[i] < reach]
        pool, left = sum([loads[i] for i in movable]), rest
        for i in movable:
            extra = min(reach - given[i], max(1, left * loads[i] // pool), rest)
            given[i] = given[i] + extra
            rest = rest - extra
    return np.array(given)


def normal_values(key, shape, spread, most, split=(), kind=jnp.bfloat16):
    loudness = shard_levels(key, shape, split, -0.22, 0.18) if split else 1.0
    array = jax.random.normal(key, shape, jnp.float32) * spread * loudness
    return jnp.minimum(jnp.maximum(array, -most), most).astype(kind)


def setup_inputs(seed: int = 0) -> dict:
    key_list = jax.random.split(jax.random.key(seed), 7)
    tokens = normal_values(key_list[0], (TOKENS, D), 1.0, 6.0, ((0, 16), (1, 16)))
    expert_ids_keys = jax.random.split(jax.random.fold_in(key_list[1], 1), TOKENS // TOK_DP)
    expert_ids_turns = jax.random.permutation(jax.random.fold_in(key_list[1], 3), TOKENS // TOK_DP)
    expert_ids = jax.vmap(lambda own, number: routed_block(jax.random.fold_in(key_list[1], 2), own, number, TOK_DP, EXPERTS, 2, CAP, 2))(expert_ids_keys, expert_ids_turns).reshape((TOKENS, 2))
    gate_levels = touch_ends(jax.random.randint(key_list[2], (TOKENS, 2), 1, 256), jax.random.fold_in(key_list[2], 1), 1, 255).astype(jnp.int32)
    w_gate = normal_values(key_list[3], (D, EXPERTS * FF), D ** -0.5, 0.09375, ((1, 256),))
    w_up = normal_values(key_list[4], (D, EXPERTS * FF), D ** -0.5, 0.09375, ((1, 256),))
    w_down = normal_values(key_list[5], (EXPERTS * FF, D), FF ** -0.5, 0.046875, ((0, 256),))
    return dict(tokens=tokens, expert_ids=expert_ids, gate_levels=gate_levels, w_gate=w_gate, w_up=w_up, w_down=w_down)


def reference(tokens, expert_ids, gate_levels, w_gate, w_up, w_down):
    levels = gate_levels.astype(jnp.float32)
    gate_frac = levels / jnp.sum(levels, axis=1, keepdims=True)
    flat_ids = expert_ids.reshape(-1)
    total = flat_ids.shape[0]
    token_of = (jnp.arange(total, dtype=jnp.int32) // 2).astype(jnp.int32)
    frac_flat = gate_frac.reshape(-1)
    limit = N_DP * CAP
    mixed_acc = jnp.zeros((TOKENS, D), jnp.float32)
    for expert in range(EXPERTS):
        keyed = (flat_ids != expert).astype(jnp.int32)
        order = jnp.argsort(keyed, stable=True)[:limit].astype(jnp.int32)
        valid = (keyed[order] == 0).astype(jnp.float32)
        rows_tok = token_of[order]
        rows = tokens[rows_tok]
        weight = frac_flat[order] * valid
        for half in range(FSPLIT):
            def block_step(index, acc):
                start = ((expert * FSPLIT + half) * N_HID + index) * FB
                g_cols = lax.dynamic_slice_in_dim(w_gate, start, FB, 1)
                u_cols = lax.dynamic_slice_in_dim(w_up, start, FB, 1)
                d_rows = lax.dynamic_slice_in_dim(w_down, start, FB, 0)
                gate = jnp.dot(rows, g_cols, preferred_element_type=jnp.float32)
                up = jnp.dot(rows, u_cols, preferred_element_type=jnp.float32)
                hidden = (jax.nn.silu(gate) * up).astype(jnp.bfloat16)
                term = jnp.dot(hidden, d_rows, preferred_element_type=jnp.float32).astype(jnp.bfloat16)
                term = lax.optimization_barrier(term)
                return acc + term.astype(jnp.float32)
            acc = lax.fori_loop(0, N_HID, block_step, jnp.zeros((limit, D), jnp.float32))
            part = lax.optimization_barrier(acc.astype(jnp.bfloat16)).astype(jnp.float32)
            mixed_acc = mixed_acc.at[rows_tok].add(weight[:, None] * part)
    return mixed_acc.astype(jnp.bfloat16)
```

```python
import jax
import jax.numpy as jnp
from jax import lax
from jax.sharding import PartitionSpec as P

EXPERTS = 8


def local(tokens, expert_ids, gate_levels, w_gate, w_up, w_down):
    devices_dp = lax.axis_size("dp")
    halves_each = devices_dp // EXPERTS
    tok_rows = expert_ids.shape[0]
    capacity = 3 * tok_rows // 8
    part_cap = capacity // halves_each
    chunk = tokens.shape[1]
    flat_ids = expert_ids.reshape(-1)
    total = flat_ids.shape[0]
    one_hot = (flat_ids[:, None] == jnp.arange(EXPERTS, dtype=jnp.int32)[None, :]).astype(jnp.int32)
    earlier = jnp.cumsum(one_hot, axis=0) - one_hot
    slot_of = jnp.sum(earlier * one_hot, axis=1)
    dest_row = flat_ids * capacity + slot_of
    src_token = (
        jnp.full((EXPERTS * capacity,), -1, jnp.int32)
        .at[dest_row]
        .set(jnp.arange(total, dtype=jnp.int32) // 2)
    )
    filled = src_token >= 0
    src_index = jnp.maximum(src_token, 0)
    levels = gate_levels.astype(jnp.float32)
    gate_frac = levels / jnp.sum(levels, axis=1, keepdims=True)

    picked = jnp.where(filled[:, None], tokens[src_index], jnp.zeros((), tokens.dtype))
    picked = picked.reshape(devices_dp, part_cap, chunk)
    received = lax.all_to_all(picked, "dp", split_axis=0, concat_axis=0, tiled=True)
    rows_mine = received.reshape(devices_dp * part_cap, chunk)
    x_mine = lax.all_gather(rows_mine, "hid", axis=1, tiled=True)

    pairs = [(i, i ^ 1) for i in range(devices_dp)]
    x_other = lax.ppermute(x_mine, "dp", pairs)

    def ffn(x):
        gate = jnp.dot(x, w_gate, preferred_element_type=jnp.float32)
        up = jnp.dot(x, w_up, preferred_element_type=jnp.float32)
        hidden = (jax.nn.silu(gate) * up).astype(jnp.bfloat16)
        return jnp.dot(hidden, w_down, preferred_element_type=jnp.float32)

    p_mine = ffn(x_mine)
    p_other = ffn(x_other).astype(jnp.bfloat16)
    p_back = lax.ppermute(p_other, "dp", pairs)
    both = (p_mine + p_back.astype(jnp.float32)).astype(jnp.bfloat16)
    summed = lax.psum_scatter(both, "hid", scatter_dimension=1, tiled=True)
    returned = lax.all_to_all(
        summed.reshape(devices_dp, part_cap, chunk), "dp", split_axis=0, concat_axis=0, tiled=True
    )
    back = returned.reshape(EXPERTS * capacity, chunk).astype(jnp.float32)
    chosen = back[dest_row] * gate_frac.reshape(-1)[:, None]
    return chosen.reshape(tok_rows, 2, chunk).sum(axis=1).astype(jnp.bfloat16)


def solution(mesh):
    placed = (
        P("dp", "hid"),
        P("dp", None),
        P("dp", None),
        P(None, ("dp", "hid")),
        P(None, ("dp", "hid")),
        P(("dp", "hid"), None),
    )
    return jax.shard_map(
        local, mesh=mesh, in_specs=placed, out_specs=P("dp", "hid"), check_vma=False
    )
```

```python
import jax
import jax.numpy as jnp
from jax import lax
from jax.sharding import PartitionSpec as P

EXPERTS = 8


def hid_rings(n_hid):
    n_z = n_hid // 2
    swap = [(h, h ^ n_z) for h in range(n_hid)]
    cw = [(h, (h // n_z) * n_z + (h % n_z + 1) % n_z) for h in range(n_hid)]
    ccw = [(h, (h // n_z) * n_z + (h % n_z - 1) % n_z) for h in range(n_hid)]
    return n_z, swap, cw, ccw


def gather_hid(x):
    n_hid = lax.axis_size("hid")
    n_z, swap, cw, ccw = hid_rings(n_hid)
    h = lax.axis_index("hid")
    z, x_lo = h % n_z, h // n_z
    y = lax.ppermute(x, "hid", swap)
    pair = jnp.where(x_lo == 0, jnp.stack([x, y], 1), jnp.stack([y, x], 1))
    rel = [pair] * n_z
    a = b = pair
    for s in range(1, n_z // 2 + 1):
        a = lax.ppermute(a, "hid", cw)
        rel[s] = a
        if s < n_z - s:
            b = lax.ppermute(b, "hid", ccw)
            rel[n_z - s] = b
    rel = jnp.stack(rel, 0)
    order = (z - jnp.arange(n_z)) % n_z
    full = jnp.take(rel, order, axis=0)
    rows, chunk = x.shape
    return full.transpose(1, 2, 0, 3).reshape(rows, n_hid * chunk)


def scatter_hid(p):
    n_hid = lax.axis_size("hid")
    n_z, swap, cw, ccw = hid_rings(n_hid)
    h = lax.axis_index("hid")
    z, x_lo = h % n_z, h // n_z
    rows = p.shape[0]
    chunk = p.shape[1] // n_hid
    half = rows // 2
    pt = p.reshape(rows, 2, n_z, chunk).transpose(2, 0, 1, 3)
    top, bottom = pt[:, :half], pt[:, half:]
    a = jnp.take(top, (z - 1) % n_z, axis=0)
    b = jnp.take(bottom, (z + 1) % n_z, axis=0)
    for s in range(n_z - 1):
        ra = lax.ppermute(a.astype(jnp.bfloat16), "hid", cw)
        rb = lax.ppermute(b.astype(jnp.bfloat16), "hid", ccw)
        a = ra.astype(jnp.float32) + jnp.take(top, (z - s - 2) % n_z, axis=0)
        b = rb.astype(jnp.float32) + jnp.take(bottom, (z + s + 2) % n_z, axis=0)
    block = jnp.concatenate([a, b], 0)
    give = jnp.where(x_lo == 0, block[:, 1], block[:, 0])
    keep = jnp.where(x_lo == 0, block[:, 0], block[:, 1])
    got = lax.ppermute(give.astype(jnp.bfloat16), "hid", swap)
    return (keep + got.astype(jnp.float32)).astype(jnp.bfloat16)


def local(tokens, expert_ids, gate_levels, w_gate, w_up, w_down):
    devices_dp = lax.axis_size("dp")
    halves_each = devices_dp // EXPERTS
    tok_rows = expert_ids.shape[0]
    capacity = 3 * tok_rows // 8
    part_cap = capacity // halves_each
    chunk = tokens.shape[1]
    flat_ids = expert_ids.reshape(-1)
    total = flat_ids.shape[0]
    one_hot = (flat_ids[:, None] == jnp.arange(EXPERTS, dtype=jnp.int32)[None, :]).astype(jnp.int32)
    earlier = jnp.cumsum(one_hot, axis=0) - one_hot
    slot_of = jnp.sum(earlier * one_hot, axis=1)
    dest_row = flat_ids * capacity + slot_of
    src_token = (
        jnp.full((EXPERTS * capacity,), -1, jnp.int32)
        .at[dest_row]
        .set(jnp.arange(total, dtype=jnp.int32) // 2)
    )
    filled = src_token >= 0
    src_index = jnp.maximum(src_token, 0)
    levels = gate_levels.astype(jnp.float32)
    gate_frac = levels / jnp.sum(levels, axis=1, keepdims=True)

    picked = jnp.where(filled[:, None], tokens[src_index], jnp.zeros((), tokens.dtype))
    picked = picked.reshape(devices_dp, part_cap, chunk)
    received = lax.all_to_all(picked, "dp", split_axis=0, concat_axis=0, tiled=True)
    rows_mine = received.reshape(devices_dp * part_cap, chunk)
    x_mine = gather_hid(rows_mine)

    pairs = [(i, i ^ 1) for i in range(devices_dp)]
    x_other = lax.ppermute(x_mine, "dp", pairs)

    def ffn(x):
        gate = jnp.dot(x, w_gate, preferred_element_type=jnp.float32)
        up = jnp.dot(x, w_up, preferred_element_type=jnp.float32)
        hidden = (jax.nn.silu(gate) * up).astype(jnp.bfloat16)
        return jnp.dot(hidden, w_down, preferred_element_type=jnp.float32)

    p_mine = ffn(x_mine)
    p_other = ffn(x_other).astype(jnp.bfloat16)
    p_back = lax.ppermute(p_other, "dp", pairs)
    both = p_mine + p_back.astype(jnp.float32)
    summed = scatter_hid(both)
    returned = lax.all_to_all(
        summed.reshape(devices_dp, part_cap, chunk), "dp", split_axis=0, concat_axis=0, tiled=True
    )
    back = returned.reshape(EXPERTS * capacity, chunk).astype(jnp.float32)
    chosen = back[dest_row] * gate_frac.reshape(-1)[:, None]
    return chosen.reshape(tok_rows, 2, chunk).sum(axis=1).astype(jnp.bfloat16)


def solution(mesh):
    placed = (
        P("dp", "hid"),
        P("dp", None),
        P("dp", None),
        P(None, ("dp", "hid")),
        P(None, ("dp", "hid")),
        P(("dp", "hid"), None),
    )
    return jax.shard_map(
        local, mesh=mesh, in_specs=placed, out_specs=P("dp", "hid"), check_vma=False
    )
```

```python
import jax
import jax.numpy as jnp
from jax import lax
from jax.sharding import PartitionSpec as P

EXPERTS = 8


def hid_rings(n_hid):
    n_z = n_hid // 2
    swap = [(h, h ^ n_z) for h in range(n_hid)]
    cw = [(h, (h // n_z) * n_z + (h % n_z + 1) % n_z) for h in range(n_hid)]
    ccw = [(h, (h // n_z) * n_z + (h % n_z - 1) % n_z) for h in range(n_hid)]
    return n_z, swap, cw, ccw


def gather_hid(x):
    n_hid = lax.axis_size("hid")
    n_z, swap, cw, ccw = hid_rings(n_hid)
    h = lax.axis_index("hid")
    z, x_lo = h % n_z, h // n_z
    y = lax.ppermute(x, "hid", swap)
    pair = jnp.where(x_lo == 0, jnp.stack([x, y], 1), jnp.stack([y, x], 1))
    rel = [pair] * n_z
    a = b = pair
    for s in range(1, n_z // 2 + 1):
        a = lax.ppermute(a, "hid", cw)
        rel[s] = a
        if s < n_z - s:
            b = lax.ppermute(b, "hid", ccw)
            rel[n_z - s] = b
    rel = jnp.stack(rel, 0)
    order = (z - jnp.arange(n_z)) % n_z
    full = jnp.take(rel, order, axis=0)
    rows, chunk = x.shape
    return full.transpose(1, 2, 0, 3).reshape(rows, n_hid * chunk)


def scatter_hid(p):
    n_hid = lax.axis_size("hid")
    n_z, swap, cw, ccw = hid_rings(n_hid)
    h = lax.axis_index("hid")
    z, x_lo = h % n_z, h // n_z
    rows = p.shape[0]
    chunk = p.shape[1] // n_hid
    half = rows // 2
    pt = p.reshape(rows, 2, n_z, chunk).transpose(2, 0, 1, 3)
    top, bottom = pt[:, :half], pt[:, half:]
    a = jnp.take(top, (z - 1) % n_z, axis=0)
    b = jnp.take(bottom, (z + 1) % n_z, axis=0)
    for s in range(n_z - 1):
        ra = lax.ppermute(a.astype(jnp.bfloat16), "hid", cw)
        rb = lax.ppermute(b.astype(jnp.bfloat16), "hid", ccw)
        a = ra.astype(jnp.float32) + jnp.take(top, (z - s - 2) % n_z, axis=0).astype(jnp.float32)
        b = rb.astype(jnp.float32) + jnp.take(bottom, (z + s + 2) % n_z, axis=0).astype(jnp.float32)
    block = jnp.concatenate([a, b], 0)
    give = jnp.where(x_lo == 0, block[:, 1], block[:, 0])
    keep = jnp.where(x_lo == 0, block[:, 0], block[:, 1])
    got = lax.ppermute(give.astype(jnp.bfloat16), "hid", swap)
    return (keep + got.astype(jnp.float32)).astype(jnp.bfloat16)


def local(tokens, expert_ids, gate_levels, w_gate, w_up, w_down):
    devices_dp = lax.axis_size("dp")
    halves_each = devices_dp // EXPERTS
    tok_rows = expert_ids.shape[0]
    capacity = 3 * tok_rows // 8
    part_cap = capacity // halves_each
    chunk = tokens.shape[1]
    flat_ids = expert_ids.reshape(-1)
    total = flat_ids.shape[0]
    one_hot = (flat_ids[:, None] == jnp.arange(EXPERTS, dtype=jnp.int32)[None, :]).astype(jnp.int32)
    earlier = jnp.cumsum(one_hot, axis=0) - one_hot
    slot_of = jnp.sum(earlier * one_hot, axis=1)
    dest_row = flat_ids * capacity + slot_of
    src_token = (
        jnp.full((EXPERTS * capacity,), -1, jnp.int32)
        .at[dest_row]
        .set(jnp.arange(total, dtype=jnp.int32) // 2)
    )
    filled = src_token >= 0
    src_index = jnp.maximum(src_token, 0)
    levels = gate_levels.astype(jnp.float32)
    gate_frac = levels / jnp.sum(levels, axis=1, keepdims=True)

    picked = jnp.where(filled[:, None], tokens[src_index], jnp.zeros((), tokens.dtype))
    picked = picked.reshape(devices_dp, part_cap, chunk)
    received = lax.all_to_all(picked, "dp", split_axis=0, concat_axis=0, tiled=True)
    rows_mine = received.reshape(devices_dp * part_cap, chunk)
    x_mine = gather_hid(rows_mine)

    pairs = [(i, i ^ 1) for i in range(devices_dp)]
    w_down_partner = lax.ppermute(w_down, "dp", pairs)
    x_other = lax.ppermute(x_mine, "dp", pairs)

    def hidden_of(x):
        gate = jnp.dot(x, w_gate, preferred_element_type=jnp.float32)
        up = jnp.dot(x, w_up, preferred_element_type=jnp.float32)
        return (jax.nn.silu(gate) * up).astype(jnp.bfloat16)

    h_mine = hidden_of(x_mine)
    h_other = hidden_of(x_other)
    h_back = lax.ppermute(h_other, "dp", pairs)
    both = jnp.dot(h_mine, w_down, preferred_element_type=jnp.float32) + jnp.dot(
        h_back, w_down_partner, preferred_element_type=jnp.float32
    )
    summed = scatter_hid(both.astype(jnp.bfloat16))
    returned = lax.all_to_all(
        summed.reshape(devices_dp, part_cap, chunk), "dp", split_axis=0, concat_axis=0, tiled=True
    )
    back = returned.reshape(EXPERTS * capacity, chunk).astype(jnp.float32)
    chosen = back[dest_row] * gate_frac.reshape(-1)[:, None]
    return chosen.reshape(tok_rows, 2, chunk).sum(axis=1).astype(jnp.bfloat16)


def solution(mesh):
    placed = (
        P("dp", "hid"),
        P("dp", None),
        P("dp", None),
        P(None, ("dp", "hid")),
        P(None, ("dp", "hid")),
        P(("dp", "hid"), None),
    )
    return jax.shard_map(
        local, mesh=mesh, in_specs=placed, out_specs=P("dp", "hid"), check_vma=False
    )
```

```python
import jax
import jax.numpy as jnp
from jax import lax
from jax.sharding import PartitionSpec as P

EXPERTS = 8


def hid_rings(n_hid):
    n_z = n_hid // 2
    swap = [(h, h ^ n_z) for h in range(n_hid)]
    cw = [(h, (h // n_z) * n_z + (h % n_z + 1) % n_z) for h in range(n_hid)]
    ccw = [(h, (h // n_z) * n_z + (h % n_z - 1) % n_z) for h in range(n_hid)]
    return n_z, swap, cw, ccw


def gather_hid(x):
    n_hid = lax.axis_size("hid")
    n_z, swap, cw, ccw = hid_rings(n_hid)
    h = lax.axis_index("hid")
    z, x_lo = h % n_z, h // n_z
    y = lax.ppermute(x, "hid", swap)
    pair = jnp.where(x_lo == 0, jnp.stack([x, y], 1), jnp.stack([y, x], 1))
    rel = [pair] * n_z
    a = b = pair
    for s in range(1, n_z // 2 + 1):
        a = lax.ppermute(a, "hid", cw)
        rel[s] = a
        if s < n_z - s:
            b = lax.ppermute(b, "hid", ccw)
            rel[n_z - s] = b
    rel = jnp.stack(rel, 0)
    order = (z - jnp.arange(n_z)) % n_z
    full = jnp.take(rel, order, axis=0)
    rows, chunk = x.shape
    return full.transpose(1, 2, 0, 3).reshape(rows, n_hid * chunk)


def scatter_hid(h_own, w_own, h_partner, w_partner):
    n_hid = lax.axis_size("hid")
    n_z, swap, cw, ccw = hid_rings(n_hid)
    h = lax.axis_index("hid")
    z, x_lo = h % n_z, h // n_z
    rows, inner = h_own.shape
    chunk = w_own.shape[-1]
    half = rows // 2
    wo, wp = w_own, w_partner

    def block(ops, lo, hi, zz):
        ho, hp = ops
        a = lax.dynamic_index_in_dim(wo, zz, axis=0, keepdims=False).reshape(inner, 2 * chunk)
        b = lax.dynamic_index_in_dim(wp, zz, axis=0, keepdims=False).reshape(wp.shape[1], 2 * chunk)
        out = jnp.dot(ho[lo:hi], a, preferred_element_type=jnp.float32) + jnp.dot(
            hp[lo:hi], b, preferred_element_type=jnp.float32
        )
        return out.reshape(hi - lo, 2, chunk)

    ops = (h_own, h_partner)
    a = block(ops, 0, half, (z - 1) % n_z)
    b = block(ops, half, rows, (z + 1) % n_z)
    for s in range(n_z - 1):
        send_a, send_b = a.astype(jnp.bfloat16), b.astype(jnp.bfloat16)
        ra = lax.ppermute(send_a, "hid", cw)
        rb = lax.ppermute(send_b, "hid", ccw)
        *ops, _, _ = lax.optimization_barrier((*ops, send_a, send_b))
        a = ra.astype(jnp.float32) + block(ops, 0, half, (z - s - 2) % n_z)
        b = rb.astype(jnp.float32) + block(ops, half, rows, (z + s + 2) % n_z)
    full = jnp.concatenate([a, b], 0)
    give = jnp.where(x_lo == 0, full[:, 1], full[:, 0])
    keep = jnp.where(x_lo == 0, full[:, 0], full[:, 1])
    got = lax.ppermute(give.astype(jnp.bfloat16), "hid", swap)
    return (keep + got.astype(jnp.float32)).astype(jnp.bfloat16)


def local(tokens, expert_ids, gate_levels, w_gate, w_up, w_down):
    devices_dp = lax.axis_size("dp")
    halves_each = devices_dp // EXPERTS
    tok_rows = expert_ids.shape[0]
    capacity = 3 * tok_rows // 8
    part_cap = capacity // halves_each
    chunk = tokens.shape[1]
    flat_ids = expert_ids.reshape(-1)
    total = flat_ids.shape[0]
    one_hot = (flat_ids[:, None] == jnp.arange(EXPERTS, dtype=jnp.int32)[None, :]).astype(jnp.int32)
    earlier = jnp.cumsum(one_hot, axis=0) - one_hot
    slot_of = jnp.sum(earlier * one_hot, axis=1)
    dest_row = flat_ids * capacity + slot_of
    src_token = (
        jnp.full((EXPERTS * capacity,), -1, jnp.int32)
        .at[dest_row]
        .set(jnp.arange(total, dtype=jnp.int32) // 2)
    )
    filled = src_token >= 0
    src_index = jnp.maximum(src_token, 0)
    levels = gate_levels.astype(jnp.float32)
    gate_frac = levels / jnp.sum(levels, axis=1, keepdims=True)

    picked = jnp.where(filled[:, None], tokens[src_index], jnp.zeros((), tokens.dtype))
    picked = picked.reshape(devices_dp, part_cap, chunk)
    received = lax.all_to_all(picked, "dp", split_axis=0, concat_axis=0, tiled=True)
    rows_mine = received.reshape(devices_dp * part_cap, chunk)
    x_mine = gather_hid(rows_mine)

    pairs = [(i, i ^ 1) for i in range(devices_dp)]
    n_z = lax.axis_size("hid") // 2
    w_down_z = w_down.reshape(w_down.shape[0], 2, n_z, chunk).transpose(2, 0, 1, 3)
    w_down_partner = lax.ppermute(w_down_z, "dp", pairs)
    x_other = lax.ppermute(x_mine, "dp", pairs)

    def hidden_of(x):
        gate = jnp.dot(x, w_gate, preferred_element_type=jnp.float32)
        up = jnp.dot(x, w_up, preferred_element_type=jnp.float32)
        return (jax.nn.silu(gate) * up).astype(jnp.bfloat16)

    h_mine = hidden_of(x_mine)
    h_other = hidden_of(x_other)
    h_back = lax.ppermute(h_other, "dp", pairs)
    summed = scatter_hid(h_mine, w_down_z, h_back, w_down_partner)
    returned = lax.all_to_all(
        summed.reshape(devices_dp, part_cap, chunk), "dp", split_axis=0, concat_axis=0, tiled=True
    )
    back = returned.reshape(EXPERTS * capacity, chunk).astype(jnp.float32)
    chosen = back[dest_row] * gate_frac.reshape(-1)[:, None]
    return chosen.reshape(tok_rows, 2, chunk).sum(axis=1).astype(jnp.bfloat16)


def solution(mesh):
    placed = (
        P("dp", "hid"),
        P("dp", None),
        P("dp", None),
        P(None, ("dp", "hid")),
        P(None, ("dp", "hid")),
        P(("dp", "hid"), None),
    )
    return jax.shard_map(
        local, mesh=mesh, in_specs=placed, out_specs=P("dp", "hid"), check_vma=False
    )
```

```python
import jax
import jax.numpy as jnp
from jax import lax
from jax.sharding import PartitionSpec as P

EXPERTS = 8


def hid_rings(n_hid):
    n_z = n_hid // 2
    swap = [(h, h ^ n_z) for h in range(n_hid)]
    cw = [(h, (h // n_z) * n_z + (h % n_z + 1) % n_z) for h in range(n_hid)]
    ccw = [(h, (h // n_z) * n_z + (h % n_z - 1) % n_z) for h in range(n_hid)]
    return n_z, swap, cw, ccw


def gather_hid(x):
    n_hid = lax.axis_size("hid")
    n_z, swap, cw, ccw = hid_rings(n_hid)
    h = lax.axis_index("hid")
    z, x_lo = h % n_z, h // n_z
    y = lax.ppermute(x, "hid", swap)
    pair = jnp.where(x_lo == 0, jnp.stack([x, y], 1), jnp.stack([y, x], 1))
    rel = [pair] * n_z
    a = b = pair
    for s in range(1, n_z // 2 + 1):
        a = lax.ppermute(a, "hid", cw)
        rel[s] = a
        if s < n_z - s:
            b = lax.ppermute(b, "hid", ccw)
            rel[n_z - s] = b
    rel = jnp.stack(rel, 0)
    order = (z - jnp.arange(n_z)) % n_z
    full = jnp.take(rel, order, axis=0)
    rows, chunk = x.shape
    return full.transpose(1, 2, 0, 3).reshape(rows, n_hid * chunk)


def scatter_hid(p):
    n_hid = lax.axis_size("hid")
    n_z, swap, cw, ccw = hid_rings(n_hid)
    h = lax.axis_index("hid")
    z, x_lo = h % n_z, h // n_z
    rows = p.shape[0]
    chunk = p.shape[1] // n_hid
    half = rows // 2
    pt = p.reshape(rows, 2, n_z, chunk).transpose(2, 0, 1, 3)
    top, bottom = pt[:, :half], pt[:, half:]
    a = jnp.take(top, (z - 1) % n_z, axis=0)
    b = jnp.take(bottom, (z + 1) % n_z, axis=0)
    def step(s, carry):
        a, b = carry
        ra = lax.ppermute(a.astype(jnp.bfloat16), "hid", cw)
        rb = lax.ppermute(b.astype(jnp.bfloat16), "hid", ccw)
        a = ra.astype(jnp.float32) + lax.dynamic_index_in_dim(top, (z - s - 2) % n_z, 0, False).astype(jnp.float32)
        b = rb.astype(jnp.float32) + lax.dynamic_index_in_dim(bottom, (z + s + 2) % n_z, 0, False).astype(jnp.float32)
        return a, b

    a, b = lax.fori_loop(0, n_z - 1, step, (a.astype(jnp.float32), b.astype(jnp.float32)))
    block = jnp.concatenate([a, b], 0)
    give = jnp.where(x_lo == 0, block[:, 1], block[:, 0])
    keep = jnp.where(x_lo == 0, block[:, 0], block[:, 1])
    got = lax.ppermute(give.astype(jnp.bfloat16), "hid", swap)
    return (keep + got.astype(jnp.float32)).astype(jnp.bfloat16)


def local(tokens, expert_ids, gate_levels, w_gate, w_up, w_down):
    devices_dp = lax.axis_size("dp")
    halves_each = devices_dp // EXPERTS
    tok_rows = expert_ids.shape[0]
    capacity = 3 * tok_rows // 8
    part_cap = capacity // halves_each
    chunk = tokens.shape[1]
    flat_ids = expert_ids.reshape(-1)
    total = flat_ids.shape[0]
    one_hot = (flat_ids[:, None] == jnp.arange(EXPERTS, dtype=jnp.int32)[None, :]).astype(jnp.int32)
    earlier = jnp.cumsum(one_hot, axis=0) - one_hot
    slot_of = jnp.sum(earlier * one_hot, axis=1)
    dest_row = flat_ids * capacity + slot_of
    src_token = (
        jnp.full((EXPERTS * capacity,), -1, jnp.int32)
        .at[dest_row]
        .set(jnp.arange(total, dtype=jnp.int32) // 2)
    )
    filled = src_token >= 0
    src_index = jnp.maximum(src_token, 0)
    levels = gate_levels.astype(jnp.float32)
    gate_frac = levels / jnp.sum(levels, axis=1, keepdims=True)

    picked = jnp.where(filled[:, None], tokens[src_index], jnp.zeros((), tokens.dtype))
    picked = picked.reshape(devices_dp, part_cap, chunk)
    received = lax.all_to_all(picked, "dp", split_axis=0, concat_axis=0, tiled=True)
    rows_mine = received.reshape(devices_dp * part_cap, chunk)
    x_mine = gather_hid(rows_mine)

    pairs = [(i, i ^ 1) for i in range(devices_dp)]
    w_down_partner = lax.ppermute(w_down, "dp", pairs)
    x_other = lax.ppermute(x_mine, "dp", pairs)

    def hidden_of(x):
        gate = jnp.dot(x, w_gate, preferred_element_type=jnp.float32)
        up = jnp.dot(x, w_up, preferred_element_type=jnp.float32)
        return (jax.nn.silu(gate) * up).astype(jnp.bfloat16)

    h_mine = hidden_of(x_mine)
    h_other = hidden_of(x_other)
    h_back = lax.ppermute(h_other, "dp", pairs)
    both = jnp.dot(h_mine, w_down, preferred_element_type=jnp.float32) + jnp.dot(
        h_back, w_down_partner, preferred_element_type=jnp.float32
    )
    summed = scatter_hid(both.astype(jnp.bfloat16))
    returned = lax.all_to_all(
        summed.reshape(devices_dp, part_cap, chunk), "dp", split_axis=0, concat_axis=0, tiled=True
    )
    back = returned.reshape(EXPERTS * capacity, chunk).astype(jnp.float32)
    chosen = back[dest_row] * gate_frac.reshape(-1)[:, None]
    return chosen.reshape(tok_rows, 2, chunk).sum(axis=1).astype(jnp.bfloat16)


def solution(mesh):
    placed = (
        P("dp", "hid"),
        P("dp", None),
        P("dp", None),
        P(None, ("dp", "hid")),
        P(None, ("dp", "hid")),
        P(("dp", "hid"), None),
    )
    return jax.shard_map(
        local, mesh=mesh, in_specs=placed, out_specs=P("dp", "hid"), check_vma=False
    )
```

```python
import jax
import jax.numpy as jnp
from jax import lax
from jax.sharding import PartitionSpec as P

EXPERTS = 8


def hid_rings(n_hid):
    n_z = n_hid // 2
    swap = [(h, h ^ n_z) for h in range(n_hid)]
    cw = [(h, (h // n_z) * n_z + (h % n_z + 1) % n_z) for h in range(n_hid)]
    ccw = [(h, (h // n_z) * n_z + (h % n_z - 1) % n_z) for h in range(n_hid)]
    return n_z, swap, cw, ccw


def gather_hid(x):
    n_hid = lax.axis_size("hid")
    n_z, swap, cw, ccw = hid_rings(n_hid)
    h = lax.axis_index("hid")
    z, x_lo = h % n_z, h // n_z
    rows, chunk = x.shape
    y = lax.ppermute(x, "hid", swap)
    full = jnp.zeros((rows, 2, n_z, chunk), x.dtype)

    def place(full, pair, zz):
        full = lax.dynamic_update_slice(full, pair[:, 0][:, None, None], (0, x_lo, zz, 0))
        return lax.dynamic_update_slice(full, pair[:, 1][:, None, None], (0, 1 - x_lo, zz, 0))

    pair = jnp.stack([x, y], 1)
    full = place(full, pair, z)
    a = b = pair
    for s in range(1, n_z // 2 + 1):
        a = lax.ppermute(a, "hid", cw)
        full = place(full, a, (z - s) % n_z)
        if s < n_z - s:
            b = lax.ppermute(b, "hid", ccw)
            full = place(full, b, (z + s) % n_z)
    return full.reshape(rows, n_hid * chunk)


def scatter_hid(p):
    n_hid = lax.axis_size("hid")
    n_z, swap, cw, ccw = hid_rings(n_hid)
    h = lax.axis_index("hid")
    z, x_lo = h % n_z, h // n_z
    rows = p.shape[0]
    chunk = p.shape[1] // n_hid
    half = rows // 2
    pt = p.reshape(rows, 2, n_z, chunk).transpose(2, 0, 1, 3)
    top, bottom = pt[:, :half], pt[:, half:]
    a = jnp.take(top, (z - 1) % n_z, axis=0)
    b = jnp.take(bottom, (z + 1) % n_z, axis=0)
    for s in range(n_z - 1):
        ra = lax.ppermute(a.astype(jnp.bfloat16), "hid", cw)
        rb = lax.ppermute(b.astype(jnp.bfloat16), "hid", ccw)
        a = ra.astype(jnp.float32) + jnp.take(top, (z - s - 2) % n_z, axis=0).astype(jnp.float32)
        b = rb.astype(jnp.float32) + jnp.take(bottom, (z + s + 2) % n_z, axis=0).astype(jnp.float32)
    block = jnp.concatenate([a, b], 0)
    give = jnp.where(x_lo == 0, block[:, 1], block[:, 0])
    keep = jnp.where(x_lo == 0, block[:, 0], block[:, 1])
    got = lax.ppermute(give.astype(jnp.bfloat16), "hid", swap)
    return (keep + got.astype(jnp.float32)).astype(jnp.bfloat16)


def local(tokens, expert_ids, gate_levels, w_gate, w_up, w_down):
    devices_dp = lax.axis_size("dp")
    halves_each = devices_dp // EXPERTS
    tok_rows = expert_ids.shape[0]
    capacity = 3 * tok_rows // 8
    part_cap = capacity // halves_each
    chunk = tokens.shape[1]
    flat_ids = expert_ids.reshape(-1)
    total = flat_ids.shape[0]
    one_hot = (flat_ids[:, None] == jnp.arange(EXPERTS, dtype=jnp.int32)[None, :]).astype(jnp.int32)
    earlier = jnp.cumsum(one_hot, axis=0) - one_hot
    slot_of = jnp.sum(earlier * one_hot, axis=1)
    dest_row = flat_ids * capacity + slot_of
    src_token = (
        jnp.full((EXPERTS * capacity,), -1, jnp.int32)
        .at[dest_row]
        .set(jnp.arange(total, dtype=jnp.int32) // 2)
    )
    filled = src_token >= 0
    src_index = jnp.maximum(src_token, 0)
    levels = gate_levels.astype(jnp.float32)
    gate_frac = levels / jnp.sum(levels, axis=1, keepdims=True)

    picked = jnp.where(filled[:, None], tokens[src_index], jnp.zeros((), tokens.dtype))
    picked = picked.reshape(devices_dp, part_cap, chunk)
    received = lax.all_to_all(picked, "dp", split_axis=0, concat_axis=0, tiled=True)
    rows_mine = received.reshape(devices_dp * part_cap, chunk)
    x_mine = gather_hid(rows_mine)

    pairs = [(i, i ^ 1) for i in range(devices_dp)]
    w_down_partner = lax.ppermute(w_down, "dp", pairs)
    x_other = lax.ppermute(x_mine, "dp", pairs)

    def hidden_of(x):
        gate = jnp.dot(x, w_gate, preferred_element_type=jnp.float32)
        up = jnp.dot(x, w_up, preferred_element_type=jnp.float32)
        return (jax.nn.silu(gate) * up).astype(jnp.bfloat16)

    h_mine = hidden_of(x_mine)
    h_other = hidden_of(x_other)
    h_back = lax.ppermute(h_other, "dp", pairs)
    both = jnp.dot(h_mine, w_down, preferred_element_type=jnp.float32) + jnp.dot(
        h_back, w_down_partner, preferred_element_type=jnp.float32
    )
    summed = scatter_hid(both.astype(jnp.bfloat16))
    returned = lax.all_to_all(
        summed.reshape(devices_dp, part_cap, chunk), "dp", split_axis=0, concat_axis=0, tiled=True
    )
    back = returned.reshape(EXPERTS * capacity, chunk).astype(jnp.float32)
    chosen = back[dest_row] * gate_frac.reshape(-1)[:, None]
    return chosen.reshape(tok_rows, 2, chunk).sum(axis=1).astype(jnp.bfloat16)


def solution(mesh):
    placed = (
        P("dp", "hid"),
        P("dp", None),
        P("dp", None),
        P(None, ("dp", "hid")),
        P(None, ("dp", "hid")),
        P(("dp", "hid"), None),
    )
    return jax.shard_map(
        local, mesh=mesh, in_specs=placed, out_specs=P("dp", "hid"), check_vma=False
    )
```

```python
import jax
import jax.numpy as jnp
from jax import lax
from jax.sharding import PartitionSpec as P

EXPERTS = 8


def hid_rings(n_hid):
    n_z = n_hid // 2
    swap = [(h, h ^ n_z) for h in range(n_hid)]
    cw = [(h, (h // n_z) * n_z + (h % n_z + 1) % n_z) for h in range(n_hid)]
    ccw = [(h, (h // n_z) * n_z + (h % n_z - 1) % n_z) for h in range(n_hid)]
    return n_z, swap, cw, ccw


def gather_hid(x):
    n_hid = lax.axis_size("hid")
    n_z, swap, cw, ccw = hid_rings(n_hid)
    h = lax.axis_index("hid")
    z, x_lo = h % n_z, h // n_z
    n_cw = n_z // 2
    n_ccw = n_z - 1 - n_cw
    own = [x] * n_z
    other = [x] * n_z
    other[0] = lax.ppermute(x, "hid", swap)
    a = lax.ppermute(x, "hid", cw)
    b = lax.ppermute(x, "hid", ccw)
    own[1], own[n_z - 1] = a, b
    for k in range(2, n_cw + 2):
        if k <= n_cw:
            got = lax.ppermute(jnp.stack([own[k - 1], other[k - 2]], 0), "hid", cw)
            own[k], other[k - 1] = got[0], got[1]
        else:
            other[k - 1] = lax.ppermute(other[k - 2], "hid", cw)
        if k <= n_ccw:
            got = lax.ppermute(jnp.stack([own[n_z - k + 1], other[(n_z - k + 2) % n_z]], 0), "hid", ccw)
            own[n_z - k], other[n_z - k + 1] = got[0], got[1]
        elif k == n_ccw + 1:
            other[n_z - k + 1] = lax.ppermute(other[(n_z - k + 2) % n_z], "hid", ccw)
    rel = jnp.stack([jnp.stack(own, 0), jnp.stack(other, 0)], 2)
    rel = jnp.where(x_lo == 0, rel, rel[:, :, ::-1])
    order = (z - jnp.arange(n_z)) % n_z
    full = jnp.take(rel, order, axis=0)
    rows, chunk = x.shape
    return full.transpose(1, 2, 0, 3).reshape(rows, n_hid * chunk)


def scatter_hid(p):
    n_hid = lax.axis_size("hid")
    n_z, swap, cw, ccw = hid_rings(n_hid)
    h = lax.axis_index("hid")
    z, x_lo = h % n_z, h // n_z
    rows = p.shape[0]
    chunk = p.shape[1] // n_hid
    half = rows // 2
    pt = p.reshape(rows, 2, n_z, chunk).transpose(2, 0, 1, 3)
    top, bottom = pt[:, :half], pt[:, half:]
    a = jnp.take(top, (z - 1) % n_z, axis=0)
    b = jnp.take(bottom, (z + 1) % n_z, axis=0)
    for s in range(n_z - 1):
        ra = lax.ppermute(a.astype(jnp.bfloat16), "hid", cw)
        rb = lax.ppermute(b.astype(jnp.bfloat16), "hid", ccw)
        a = ra.astype(jnp.float32) + jnp.take(top, (z - s - 2) % n_z, axis=0).astype(jnp.float32)
        b = rb.astype(jnp.float32) + jnp.take(bottom, (z + s + 2) % n_z, axis=0).astype(jnp.float32)
    block = jnp.concatenate([a, b], 0)
    give = jnp.where(x_lo == 0, block[:, 1], block[:, 0])
    keep = jnp.where(x_lo == 0, block[:, 0], block[:, 1])
    got = lax.ppermute(give.astype(jnp.bfloat16), "hid", swap)
    return (keep + got.astype(jnp.float32)).astype(jnp.bfloat16)


def local(tokens, expert_ids, gate_levels, w_gate, w_up, w_down):
    devices_dp = lax.axis_size("dp")
    halves_each = devices_dp // EXPERTS
    tok_rows = expert_ids.shape[0]
    capacity = 3 * tok_rows // 8
    part_cap = capacity // halves_each
    chunk = tokens.shape[1]
    flat_ids = expert_ids.reshape(-1)
    total = flat_ids.shape[0]
    one_hot = (flat_ids[:, None] == jnp.arange(EXPERTS, dtype=jnp.int32)[None, :]).astype(jnp.int32)
    earlier = jnp.cumsum(one_hot, axis=0) - one_hot
    slot_of = jnp.sum(earlier * one_hot, axis=1)
    dest_row = flat_ids * capacity + slot_of
    src_token = (
        jnp.full((EXPERTS * capacity,), -1, jnp.int32)
        .at[dest_row]
        .set(jnp.arange(total, dtype=jnp.int32) // 2)
    )
    filled = src_token >= 0
    src_index = jnp.maximum(src_token, 0)
    levels = gate_levels.astype(jnp.float32)
    gate_frac = levels / jnp.sum(levels, axis=1, keepdims=True)

    picked = jnp.where(filled[:, None], tokens[src_index], jnp.zeros((), tokens.dtype))
    picked = picked.reshape(devices_dp, part_cap, chunk)
    received = lax.all_to_all(picked, "dp", split_axis=0, concat_axis=0, tiled=True)
    rows_mine = received.reshape(devices_dp * part_cap, chunk)
    x_mine = gather_hid(rows_mine)

    pairs = [(i, i ^ 1) for i in range(devices_dp)]
    w_down_partner = lax.ppermute(w_down, "dp", pairs)
    x_other = lax.ppermute(x_mine, "dp", pairs)

    def hidden_of(x):
        gate = jnp.dot(x, w_gate, preferred_element_type=jnp.float32)
        up = jnp.dot(x, w_up, preferred_element_type=jnp.float32)
        return (jax.nn.silu(gate) * up).astype(jnp.bfloat16)

    h_mine = hidden_of(x_mine)
    h_other = hidden_of(x_other)
    h_back = lax.ppermute(h_other, "dp", pairs)
    both = jnp.dot(h_mine, w_down, preferred_element_type=jnp.float32) + jnp.dot(
        h_back, w_down_partner, preferred_element_type=jnp.float32
    )
    summed = scatter_hid(both.astype(jnp.bfloat16))
    returned = lax.all_to_all(
        summed.reshape(devices_dp, part_cap, chunk), "dp", split_axis=0, concat_axis=0, tiled=True
    )
    back = returned.reshape(EXPERTS * capacity, chunk).astype(jnp.float32)
    chosen = back[dest_row] * gate_frac.reshape(-1)[:, None]
    return chosen.reshape(tok_rows, 2, chunk).sum(axis=1).astype(jnp.bfloat16)


def solution(mesh):
    placed = (
        P("dp", "hid"),
        P("dp", None),
        P("dp", None),
        P(None, ("dp", "hid")),
        P(None, ("dp", "hid")),
        P(("dp", "hid"), None),
    )
    return jax.shard_map(
        local, mesh=mesh, in_specs=placed, out_specs=P("dp", "hid"), check_vma=False
    )
```

```python
import jax
import jax.numpy as jnp
from jax import lax
from jax.sharding import PartitionSpec as P

EXPERTS = 8


def hid_rings(n_hid):
    n_z = n_hid // 2
    swap = [(h, h ^ n_z) for h in range(n_hid)]
    cw = [(h, (h // n_z) * n_z + (h % n_z + 1) % n_z) for h in range(n_hid)]
    ccw = [(h, (h // n_z) * n_z + (h % n_z - 1) % n_z) for h in range(n_hid)]
    return n_z, swap, cw, ccw


def gather_hid(x):
    n_hid = lax.axis_size("hid")
    n_z, swap, cw, ccw = hid_rings(n_hid)
    h = lax.axis_index("hid")
    z, x_lo = h % n_z, h // n_z
    y = lax.ppermute(x, "hid", swap)
    pair = jnp.where(x_lo == 0, jnp.stack([x, y], 1), jnp.stack([y, x], 1))
    rel = [pair] * n_z
    a = b = pair
    for s in range(1, n_z // 2 + 1):
        a = lax.ppermute(a, "hid", cw)
        rel[s] = a
        if s < n_z - s:
            b = lax.ppermute(b, "hid", ccw)
            rel[n_z - s] = b
    rel = jnp.stack(rel, 0)
    order = (z - jnp.arange(n_z)) % n_z
    full = jnp.take(rel, order, axis=0)
    rows, chunk = x.shape
    return full.transpose(1, 2, 0, 3).reshape(rows, n_hid * chunk)


def scatter_hid(p):
    n_hid = lax.axis_size("hid")
    n_z, swap, cw, ccw = hid_rings(n_hid)
    h = lax.axis_index("hid")
    z, x_lo = h % n_z, h // n_z
    rows = p.shape[0]
    chunk = p.shape[1] // n_hid
    half = rows // 2
    pt = p.reshape(rows, 2, n_z, chunk).transpose(2, 0, 1, 3)
    top, bottom = pt[:, :half], pt[:, half:]
    a = jnp.take(top, (z - 1) % n_z, axis=0)
    b = jnp.take(bottom, (z + 1) % n_z, axis=0)
    for s in range(n_z - 1):
        ra = lax.ppermute(a.astype(jnp.bfloat16), "hid", cw)
        rb = lax.ppermute(b.astype(jnp.bfloat16), "hid", ccw)
        a = ra.astype(jnp.float32) + jnp.take(top, (z - s - 2) % n_z, axis=0).astype(jnp.float32)
        b = rb.astype(jnp.float32) + jnp.take(bottom, (z + s + 2) % n_z, axis=0).astype(jnp.float32)
    block = jnp.concatenate([a, b], 0)
    give = jnp.where(x_lo == 0, block[:, 1], block[:, 0])
    keep = jnp.where(x_lo == 0, block[:, 0], block[:, 1])
    got = lax.ppermute(give.astype(jnp.bfloat16), "hid", swap)
    return (keep + got.astype(jnp.float32)).astype(jnp.bfloat16)


def local(tokens, expert_ids, gate_levels, w_gate, w_up, w_down):
    devices_dp = lax.axis_size("dp")
    halves_each = devices_dp // EXPERTS
    tok_rows = expert_ids.shape[0]
    capacity = 3 * tok_rows // 8
    part_cap = capacity // halves_each
    chunk = tokens.shape[1]
    flat_ids = expert_ids.reshape(-1)
    total = flat_ids.shape[0]
    one_hot = (flat_ids[:, None] == jnp.arange(EXPERTS, dtype=jnp.int32)[None, :]).astype(jnp.int32)
    earlier = jnp.cumsum(one_hot, axis=0) - one_hot
    slot_of = jnp.sum(earlier * one_hot, axis=1)
    dest_row = flat_ids * capacity + slot_of
    src_token = (
        jnp.full((EXPERTS * capacity,), -1, jnp.int32)
        .at[dest_row]
        .set(jnp.arange(total, dtype=jnp.int32) // 2)
    )
    filled = src_token >= 0
    src_index = jnp.maximum(src_token, 0)
    levels = gate_levels.astype(jnp.float32)
    gate_frac = levels / jnp.sum(levels, axis=1, keepdims=True)

    picked = jnp.where(filled[:, None], tokens[src_index], jnp.zeros((), tokens.dtype))
    picked = picked.reshape(devices_dp, part_cap, chunk)
    received = lax.all_to_all(picked, "dp", split_axis=0, concat_axis=0, tiled=True)
    rows_mine = received.reshape(devices_dp * part_cap, chunk)
    x_mine = gather_hid(rows_mine)

    pairs = [(i, i ^ 1) for i in range(devices_dp)]
    w_down_partner = lax.ppermute(w_down, "dp", pairs)
    x_other = lax.ppermute(x_mine, "dp", pairs)

    def hidden_of(x):
        gate = jnp.dot(x, w_gate, preferred_element_type=jnp.float32)
        up = jnp.dot(x, w_up, preferred_element_type=jnp.float32)
        return (jax.nn.silu(gate) * up).astype(jnp.bfloat16)

    h_mine = hidden_of(x_mine)
    h_other = hidden_of(x_other)
    h_back = lax.ppermute(h_other, "dp", pairs)
    p_own = lax.optimization_barrier(jnp.dot(h_mine, w_down, preferred_element_type=jnp.float32).astype(jnp.bfloat16))
    both = p_own.astype(jnp.float32) + jnp.dot(h_back, w_down_partner, preferred_element_type=jnp.float32)
    summed = scatter_hid(both.astype(jnp.bfloat16))
    returned = lax.all_to_all(
        summed.reshape(devices_dp, part_cap, chunk), "dp", split_axis=0, concat_axis=0, tiled=True
    )
    back = returned.reshape(EXPERTS * capacity, chunk).astype(jnp.float32)
    chosen = back[dest_row] * gate_frac.reshape(-1)[:, None]
    return chosen.reshape(tok_rows, 2, chunk).sum(axis=1).astype(jnp.bfloat16)


def solution(mesh):
    placed = (
        P("dp", "hid"),
        P("dp", None),
        P("dp", None),
        P(None, ("dp", "hid")),
        P(None, ("dp", "hid")),
        P(("dp", "hid"), None),
    )
    return jax.shard_map(
        local, mesh=mesh, in_specs=placed, out_specs=P("dp", "hid"), check_vma=False
    )
```

```python
import jax
import jax.numpy as jnp
from jax import lax
from jax.sharding import PartitionSpec as P

EXPERTS = 8


def hid_rings(n_hid):
    n_z = n_hid // 2
    swap = [(h, h ^ n_z) for h in range(n_hid)]
    cw = [(h, (h // n_z) * n_z + (h % n_z + 1) % n_z) for h in range(n_hid)]
    ccw = [(h, (h // n_z) * n_z + (h % n_z - 1) % n_z) for h in range(n_hid)]
    return n_z, swap, cw, ccw


def gather_hid(x):
    n_hid = lax.axis_size("hid")
    n_z, swap, cw, ccw = hid_rings(n_hid)
    h = lax.axis_index("hid")
    z, x_lo = h % n_z, h // n_z
    y = lax.ppermute(x, "hid", swap)
    pair = jnp.where(x_lo == 0, jnp.stack([x, y], 1), jnp.stack([y, x], 1))
    rel = [pair] * n_z
    a = b = pair
    for s in range(1, n_z // 2 + 1):
        a = lax.ppermute(a, "hid", cw)
        rel[s] = a
        if s < n_z - s:
            b = lax.ppermute(b, "hid", ccw)
            rel[n_z - s] = b
    rel = jnp.stack(rel, 0)
    order = (z - jnp.arange(n_z)) % n_z
    full = jnp.take(rel, order, axis=0)
    rows, chunk = x.shape
    return full.transpose(1, 2, 0, 3).reshape(rows, n_hid * chunk)


def scatter_hid(p):
    n_hid = lax.axis_size("hid")
    n_z, swap, cw, ccw = hid_rings(n_hid)
    h = lax.axis_index("hid")
    z, x_lo = h % n_z, h // n_z
    rows = p.shape[0]
    chunk = p.shape[1] // n_hid
    half = rows // 2
    pt = p.reshape(rows, 2, n_z, chunk).transpose(2, 0, 1, 3)
    top, bottom = pt[:, :half], pt[:, half:]
    a = jnp.take(top, (z - 1) % n_z, axis=0)
    b = jnp.take(bottom, (z + 1) % n_z, axis=0)
    for s in range(n_z - 1):
        ra = lax.ppermute(a.astype(jnp.bfloat16), "hid", cw)
        rb = lax.ppermute(b.astype(jnp.bfloat16), "hid", ccw)
        a = ra.astype(jnp.float32) + jnp.take(top, (z - s - 2) % n_z, axis=0).astype(jnp.float32)
        b = rb.astype(jnp.float32) + jnp.take(bottom, (z + s + 2) % n_z, axis=0).astype(jnp.float32)
    block = jnp.concatenate([a, b], 0)
    give = jnp.where(x_lo == 0, block[:, 1], block[:, 0])
    keep = jnp.where(x_lo == 0, block[:, 0], block[:, 1])
    got = lax.ppermute(give.astype(jnp.bfloat16), "hid", swap)
    return (keep + got.astype(jnp.float32)).astype(jnp.bfloat16)


def local(tokens, expert_ids, gate_levels, w_gate, w_up, w_down):
    devices_dp = lax.axis_size("dp")
    halves_each = devices_dp // EXPERTS
    tok_rows = expert_ids.shape[0]
    capacity = 3 * tok_rows // 8
    part_cap = capacity // halves_each
    chunk = tokens.shape[1]
    flat_ids = expert_ids.reshape(-1)
    total = flat_ids.shape[0]
    one_hot = (flat_ids[:, None] == jnp.arange(EXPERTS, dtype=jnp.int32)[None, :]).astype(jnp.int32)
    earlier = jnp.cumsum(one_hot, axis=0) - one_hot
    slot_of = jnp.sum(earlier * one_hot, axis=1)
    dest_row = flat_ids * capacity + slot_of
    src_token = (
        jnp.full((EXPERTS * capacity,), -1, jnp.int32)
        .at[dest_row]
        .set(jnp.arange(total, dtype=jnp.int32) // 2)
    )
    filled = src_token >= 0
    src_index = jnp.maximum(src_token, 0)
    levels = gate_levels.astype(jnp.float32)
    gate_frac = levels / jnp.sum(levels, axis=1, keepdims=True)

    picked = jnp.where(filled[:, None], tokens[src_index], jnp.zeros((), tokens.dtype))
    picked = picked.reshape(devices_dp, part_cap, chunk)
    received = lax.all_to_all(picked, "dp", split_axis=0, concat_axis=0, tiled=True)
    rows_mine = received.reshape(devices_dp * part_cap, chunk)
    x_mine = gather_hid(rows_mine)

    pairs = [(i, i ^ 1) for i in range(devices_dp)]
    w_down_partner = lax.ppermute(w_down, "dp", pairs)
    x_other = lax.ppermute(x_mine, "dp", pairs)

    def hidden_of(x):
        gate = jnp.dot(x, w_gate, preferred_element_type=jnp.float32)
        up = jnp.dot(x, w_up, preferred_element_type=jnp.float32)
        return (jax.nn.silu(gate) * up).astype(jnp.bfloat16)

    h_mine = hidden_of(x_mine)
    h_other = hidden_of(x_other)
    h_back = lax.ppermute(h_other, "dp", pairs)
    p_part = lax.optimization_barrier(
        jnp.dot(h_back, w_down_partner, preferred_element_type=jnp.float32).astype(jnp.bfloat16)
    )
    both = p_part.astype(jnp.float32) + jnp.dot(h_mine, w_down, preferred_element_type=jnp.float32)
    summed = scatter_hid(both.astype(jnp.bfloat16))
    returned = lax.all_to_all(
        summed.reshape(devices_dp, part_cap, chunk), "dp", split_axis=0, concat_axis=0, tiled=True
    )
    back = returned.reshape(EXPERTS * capacity, chunk).astype(jnp.float32)
    chosen = back[dest_row] * gate_frac.reshape(-1)[:, None]
    return chosen.reshape(tok_rows, 2, chunk).sum(axis=1).astype(jnp.bfloat16)


def solution(mesh):
    placed = (
        P("dp", "hid"),
        P("dp", None),
        P("dp", None),
        P(None, ("dp", "hid")),
        P(None, ("dp", "hid")),
        P(("dp", "hid"), None),
    )
    return jax.shard_map(
        local, mesh=mesh, in_specs=placed, out_specs=P("dp", "hid"), check_vma=False
    )
```
